32 devices in a mesh: groups: 2 (over y), expert: 4 (over z), head: 2 (over x), pair: 2 (over core).
Axes of the slice: x: 2, y: 2, z: 4, core: 2. Of those that a mesh axis runs over, the one named last changes fastest.
Arguments:
- resid: bfloat16 [1024, 4096], P(('groups', 'expert'), ('head', 'pair')), parts along dimension 0, may hold values from -12 to 12
- query: bfloat16 [1024, 4096], P(('groups', 'expert'), ('head', 'pair')), parts along dimension 0, may hold values from -48 to 48
- keyval: bfloat16 [2, 1024, 512], P(None, ('groups', 'expert'), 'head'), parts along dimension 1, may hold values from -8 to 8
- wo: bfloat16 [4096, 4096], P(('head', 'pair'), 'expert'), may hold values from -0.375 to 0.375
- norm_gain: float32 [4096], replicated, may hold values from 0.1 to 1.9
- w_gate: bfloat16 [4, 4096, 1024], P('expert', None, ('head', 'pair')), may hold values from -0.09375 to 0.09375
- w_up: bfloat16 [4, 4096, 1024], P('expert', None, ('head', 'pair')), may hold values from -0.09375 to 0.09375
- w_down: bfloat16 [4, 1024, 4096], P('expert', None, ('head', 'pair')), may hold values from -0.1875 to 0.1875
- expert_ids: int32 [1024, 2], P(('groups', 'expert')), parts along dimension 0, may hold values from 0 to 3, as said below
- slot_ids: int32 [1024, 2], P(('groups', 'expert')), parts along dimension 0, may hold values from 0 to 127, as said below
- route_weights: float32 [1024, 2], P(('groups', 'expert')), parts along dimension 0, may hold values from 0.1 to 0.6
Outputs:
- attn_hidden: bfloat16 [1024, 4096], P(('groups', 'expert'), ('head', 'pair')), parts along dimension 0
- expert_mix: bfloat16 [1024, 4096], P(('groups', 'expert'), ('head', 'pair')), parts along dimension 0
The draws below stay inside these ranges and needn't reach their ends.
There are 2 independent parts, one for each index of `groups`. The reference program is written for one: setup_inputs(seed, part) draws one part's arguments, and reference() takes and returns one part's arrays. A program takes and returns all parts, laid end to end along the dimension named above; an argument that names none is the same for every part. Nothing has to cross between parts.
Inputs may be any that keep to these rules, and one draw needn't show every extreme that they name: `expert_ids`: each token names 2 different experts. Within each aligned block of 128 tokens no expert is named more than 128 times, and one expert, the same in every block of a draw, is named exactly 128 times in every block. `slot_ids`: within each aligned block of 128 tokens the routes to one expert hold the slots 0 to their count - 1, each once.
All inputs are finite; a program needn't handle non-finite values.
Results may differ from the reference program's by a relative error of at most 0.02.
Values may be sent and summed in bfloat16 or wider, within the bound.
No kernel may reach another device: no remote copies, remote signals or barrier semaphores. Data moves between devices by JAX's collectives and lax.ppermute only.
A program may use at most 64 MiB of HBM per device.

```python
import math
import jax
import jax.numpy as jnp
from jax import lax

D = 4096
QUERY_HEADS = 32
KEY_VALUE_HEADS = 4
HEAD_WIDTH = 128
FFE = 1024
TOPK = 2
TOK_DEV = 128
IMAGE_TOKENS = 512
EXPERTS = 4
CAP = 128


def routing_tables(key):
    base_key = jax.random.fold_in(key, 11)
    hot_expert = jax.random.randint(jax.random.fold_in(base_key, 1), (), 0, EXPERTS)
    block_keys = jax.random.split(jax.random.fold_in(base_key, 2), IMAGE_TOKENS // TOK_DEV)
    route_count = TOK_DEV * TOPK

    def one_block(block_key):
        perm_key, count_key, order_key = jax.random.split(block_key, 3)
        order_perm = jax.random.permutation(perm_key, EXPERTS)
        order_perm = (order_perm - order_perm[0] + hot_expert) % EXPERTS
        pair_small = jax.random.randint(count_key, (EXPERTS // 2,), 1, CAP)
        pair_small = pair_small.at[0].set(0)
        pair_counts = jnp.stack([CAP - pair_small, pair_small], axis=1).reshape(EXPERTS).astype(jnp.int32)
        counts = jnp.zeros((EXPERTS,), jnp.int32).at[order_perm].set(pair_counts)
        starts = jnp.cumsum(counts) - counts
        labels = jnp.repeat(jnp.arange(EXPERTS, dtype=jnp.int32), counts, total_repeat_length=route_count)
        slot_vals = jnp.arange(route_count, dtype=jnp.int32) - starts[labels]
        expert_vals = labels.reshape(TOPK, TOK_DEV).T
        slot_vals = slot_vals.reshape(TOPK, TOK_DEV).T
        token_order = jax.random.permutation(order_key, TOK_DEV)
        return (expert_vals[token_order], slot_vals[token_order])
    expert_vals, slot_vals = jax.vmap(one_block)(block_keys)
    return (expert_vals.reshape(IMAGE_TOKENS, TOPK).astype(jnp.int32), slot_vals.reshape(IMAGE_TOKENS, TOPK).astype(jnp.int32))


def draw_expert_ids(key, part):
    return routing_tables(key)[0]


def draw_slot_ids(key, part):
    return routing_tables(key)[1]


def attention_tables(key):
    base_key = jax.random.fold_in(key, 23)
    query_key, key_random_seed, value_random_seed = jax.random.split(base_key, 3)
    queries = 1.5 * jax.random.truncated_normal(query_key, -4.0, 4.0, (IMAGE_TOKENS, QUERY_HEADS * HEAD_WIDTH), jnp.float32)
    every_key_row = 1.5 * jax.random.truncated_normal(key_random_seed, -4.0, 4.0, (IMAGE_TOKENS, KEY_VALUE_HEADS * HEAD_WIDTH), jnp.float32)
    every_value_row = jax.random.truncated_normal(value_random_seed, -4.0, 4.0, (IMAGE_TOKENS, KEY_VALUE_HEADS * HEAD_WIDTH), jnp.float32)
    return (queries, jnp.stack([every_key_row, every_value_row]))


def draw_query(key, part):
    return attention_tables(key)[0].astype(jnp.bfloat16)


def draw_keyval(key, part):
    return attention_tables(key)[1].astype(jnp.bfloat16)


def draw_resid(key, part):
    column_pos = jnp.arange(D, dtype=jnp.float32) / D
    noise_key = jax.random.fold_in(jax.random.fold_in(key, 31), 0)
    base_vals = jax.random.truncated_normal(noise_key, -4.0, 4.0, (IMAGE_TOKENS, D), jnp.float32)
    return (base_vals * (0.6 + 1.2 * column_pos)).astype(jnp.bfloat16)


def block_scale(own_key, dims, shards, low, high):
    level, own = 1.0, jax.random.fold_in(own_key, 6)
    for axis_at, blocks in shards:
        steps = jnp.exp(jax.random.uniform(jax.random.fold_in(own, axis_at), (blocks,), jnp.float32, low / len(shards), high / len(shards)))
        level = level * jnp.repeat(steps, dims[axis_at] // blocks).reshape([-1 if axis == axis_at else 1 for axis in range(len(dims))])
    return level


def centred(own_key, dims, scale, most, cuts=(), held_as=jnp.bfloat16):
    loudness = block_scale(own_key, dims, cuts, -0.22, 0.18) if cuts else 1.0
    result = jax.random.normal(own_key, dims, jnp.float32) * scale * loudness
    return jnp.minimum(jnp.maximum(result, -most), most).astype(held_as)


def setup_inputs(seed: int = 0, part: int = 0) -> dict:
    arg_keys = jax.random.split(jax.random.key(seed), 12)
    own_keys = jax.random.split(jax.random.fold_in(arg_keys[11], part), 12)
    resid = draw_resid(jax.random.fold_in(jax.random.fold_in(arg_keys[11], part), 71), part)
    query = draw_query(jax.random.fold_in(jax.random.fold_in(arg_keys[11], part), 71), part)
    keyval = draw_keyval(jax.random.fold_in(jax.random.fold_in(arg_keys[11], part), 71), part)
    wo = centred(arg_keys[3], (QUERY_HEADS * HEAD_WIDTH, D), (QUERY_HEADS * HEAD_WIDTH // 16) ** -0.5, 0.375, ((0, 4), (1, 4)))
    norm_gain = jnp.clip(1.0 + 0.18 * jax.random.normal(arg_keys[4], (D,), jnp.float32), 0.1, 1.9)
    w_gate = centred(arg_keys[5], (EXPERTS, D, FFE), D ** -0.5, 0.09375, ((0, 4), (2, 4)))
    w_up = centred(arg_keys[6], (EXPERTS, D, FFE), D ** -0.5, 0.09375, ((0, 4), (2, 4)))
    w_down = centred(arg_keys[7], (EXPERTS, FFE, D), FFE ** -0.5, 0.1875, ((0, 4), (2, 4)))
    expert_ids = draw_expert_ids(jax.random.fold_in(jax.random.fold_in(arg_keys[11], part), 71), part)
    slot_ids = draw_slot_ids(jax.random.fold_in(jax.random.fold_in(arg_keys[11], part), 71), part)
    route_weights = jnp.clip(0.1 + 0.5 * jax.random.uniform(own_keys[10], (IMAGE_TOKENS, TOPK), jnp.float32) ** block_scale(own_keys[10], (IMAGE_TOKENS, TOPK), ((0, 4),), -0.2, 0.2), 0.1, 0.6)
    return dict(resid=resid, query=query, keyval=keyval, wo=wo, norm_gain=norm_gain, w_gate=w_gate, w_up=w_up, w_down=w_down, expert_ids=expert_ids, slot_ids=slot_ids, route_weights=route_weights)


norm_eps = 1e-06

def reference(resid, query, keyval, wo, norm_gain, w_gate, w_up, w_down, expert_ids, slot_ids, route_weights):
    heads_per_group = QUERY_HEADS // KEY_VALUE_HEADS
    positions = jnp.arange(IMAGE_TOKENS, dtype=jnp.int32)
    causal = positions[None, :] <= positions[:, None]

    def one_head(head_index):
        kv_index = head_index // heads_per_group
        query_head = lax.dynamic_slice_in_dim(query, head_index * HEAD_WIDTH, HEAD_WIDTH, 1)
        key_head = lax.dynamic_slice_in_dim(keyval[0], kv_index * HEAD_WIDTH, HEAD_WIDTH, 1)
        value_head = lax.dynamic_slice_in_dim(keyval[1], kv_index * HEAD_WIDTH, HEAD_WIDTH, 1)
        scores = jnp.dot(query_head, key_head.T, preferred_element_type=jnp.float32) / math.sqrt(HEAD_WIDTH)
        scores = jnp.where(causal, scores, -jnp.inf)
        row_max = lax.optimization_barrier(jnp.max(scores, axis=1, keepdims=True))
        weights = jnp.where(causal, jnp.exp(scores - row_max), 0.0)
        softmax_total = lax.optimization_barrier(jnp.sum(weights, axis=1, keepdims=True))
        mixed = jnp.dot(weights.astype(jnp.bfloat16), value_head, preferred_element_type=jnp.float32)
        return (mixed / softmax_total).astype(jnp.bfloat16)
    head_outs = lax.map(one_head, jnp.arange(QUERY_HEADS, dtype=jnp.int32))
    heads_out = head_outs.transpose(1, 0, 2).reshape(IMAGE_TOKENS, QUERY_HEADS * HEAD_WIDTH)
    attn_hidden = (resid.astype(jnp.float32) + jnp.dot(heads_out, wo, preferred_element_type=jnp.float32)).astype(jnp.bfloat16)
    hidden_f32 = attn_hidden.astype(jnp.float32)
    mean_square = lax.optimization_barrier(jnp.mean(hidden_f32 * hidden_f32, axis=1, keepdims=True))
    normed = (hidden_f32 * lax.rsqrt(mean_square + norm_eps) * norm_gain).astype(jnp.bfloat16)
    block_count = IMAGE_TOKENS // TOK_DEV
    block_of = (jnp.arange(IMAGE_TOKENS, dtype=jnp.int32) // TOK_DEV)[:, None]
    buffer_row = (expert_ids * (block_count * CAP) + block_of * CAP + slot_ids).astype(jnp.int32)
    slot_rows = jnp.zeros((EXPERTS * block_count * CAP, D), jnp.bfloat16)
    slot_rows = slot_rows.at[buffer_row.reshape(-1)].set(jnp.repeat(normed, TOPK, axis=0))
    slot_rows = slot_rows.reshape(EXPERTS, block_count * CAP, D)

    def one_expert(expert_index):
        slot_block = slot_rows[expert_index]
        gate_val = jnp.dot(slot_block, w_gate[expert_index], preferred_element_type=jnp.float32)
        up_val = jnp.dot(slot_block, w_up[expert_index], preferred_element_type=jnp.float32)
        activated = (jax.nn.silu(gate_val) * up_val).astype(jnp.bfloat16)
        return jnp.dot(activated, w_down[expert_index], preferred_element_type=jnp.float32).astype(jnp.bfloat16)
    expert_out = lax.map(one_expert, jnp.arange(EXPERTS, dtype=jnp.int32)).reshape(EXPERTS * block_count * CAP, D)
    picked = expert_out[buffer_row]
    expert_mix = lax.optimization_barrier(jnp.sum(route_weights[:, :, None] * picked.astype(jnp.float32), axis=1)).astype(jnp.bfloat16)
    return (attn_hidden, expert_mix)
```

```python
import functools
import math

import jax
import jax.numpy as jnp
from jax import lax
from jax.experimental import pallas as pl
from jax.experimental.pallas import tpu as pltpu
from jax.sharding import PartitionSpec as P

D = 4096
QUERY_HEADS = 32
KEY_VALUE_HEADS = 4
HEAD_WIDTH = 128
TOPK = 2
LANES = 128

norm_eps = 1e-06
RING = ("expert", "head", "pair")


def expert_block(w_gate, w_up, w_down, slot_block):
    gate_val = jnp.einsum("ensd,edf->ensf", slot_block, w_gate, preferred_element_type=jnp.float32)
    up_val = jnp.einsum("ensd,edf->ensf", slot_block, w_up, preferred_element_type=jnp.float32)
    activated = (jax.nn.silu(gate_val) * up_val).astype(jnp.bfloat16)
    all_hidden = lax.all_gather(activated, ("head", "pair"), axis=3, tiled=True)
    return jnp.einsum(
        "ensf,efd->ensd", all_hidden, w_down, preferred_element_type=jnp.float32
    ).astype(jnp.bfloat16)


def general_body(
    resid, query, keyval, wo, norm_gain, w_gate, w_up, w_down, expert_ids, slot_ids, route_weights
):
    tok_rows = resid.shape[0]
    feature_cols = resid.shape[1]
    q_local = query.shape[1] // HEAD_WIDTH
    kv_local = keyval.shape[2] // HEAD_WIDTH
    heads_per_group = QUERY_HEADS // KEY_VALUE_HEADS
    query_pos = lax.axis_index("expert") * tok_rows + jnp.arange(tok_rows, dtype=jnp.int32)
    key_head = (
        lax.axis_index("pair") * q_local + jnp.arange(q_local, dtype=jnp.int32)
    ) // heads_per_group
    queries = query.reshape(tok_rows, q_local, HEAD_WIDTH)
    inverse_root = 1.0 / math.sqrt(HEAD_WIDTH)
    shards = lax.all_gather(keyval, "expert", axis=1, tiled=True)
    run_max = jnp.full((tok_rows, q_local), -1e30, jnp.float32)
    count = shards.shape[1]
    keys_here = jnp.take(shards[0].reshape(count, kv_local, HEAD_WIDTH), key_head, axis=1)
    values_here = jnp.take(shards[1].reshape(count, kv_local, HEAD_WIDTH), key_head, axis=1)
    scores = (
        jnp.einsum("thd,uhd->thu", queries, keys_here, preferred_element_type=jnp.float32)
        * inverse_root
    )
    key_pos = jnp.arange(count, dtype=jnp.int32)
    visible = (key_pos[None, :] <= query_pos[:, None])[:, None, :]
    scores = jnp.where(visible, scores, -jnp.inf)
    new_max = jnp.maximum(run_max, jnp.max(scores, axis=2))
    weights = jnp.where(visible, jnp.exp(scores - new_max[:, :, None]), 0.0)
    run_total = jnp.sum(weights, axis=2)
    weighted = jnp.einsum(
        "thu,uhd->thd",
        weights.astype(jnp.bfloat16),
        values_here,
        preferred_element_type=jnp.float32,
    )
    heads_out = (
        (weighted / run_total[:, :, None])
        .astype(jnp.bfloat16)
        .reshape(tok_rows, q_local * HEAD_WIDTH)
    )
    partial_proj = jnp.dot(
        heads_out,
        lax.all_gather(wo, "expert", axis=1, tiled=True),
        preferred_element_type=jnp.float32,
    )
    attn_sum = lax.psum_scatter(
        partial_proj.astype(jnp.bfloat16), ("head", "pair"), scatter_dimension=1, tiled=True
    ).astype(jnp.float32)
    attn_hidden = (resid.astype(jnp.float32) + attn_sum).astype(jnp.bfloat16)
    experts_here = w_gate.shape[0]
    experts_all = experts_here * lax.axis_size("expert")
    capacity = 2 * tok_rows * TOPK // experts_all
    target = expert_ids * capacity + slot_ids
    slot_index = jnp.arange(experts_all * capacity, dtype=jnp.int32)
    placing = jnp.sum(
        (target[None, :, :] == slot_index[:, None, None]).astype(jnp.int32), axis=2
    ).astype(jnp.bfloat16)
    row_floats = attn_hidden.astype(jnp.float32)
    square_sum = lax.psum(jnp.sum(row_floats * row_floats, axis=1), ("head", "pair"))
    mean_square = (square_sum / D)[:, None]
    shard_index = lax.axis_index("head") * lax.axis_size("pair") + lax.axis_index("pair")
    gain_part = lax.dynamic_slice_in_dim(norm_gain, shard_index * feature_cols, feature_cols)
    normed = (row_floats * lax.rsqrt(mean_square + norm_eps) * gain_part).astype(jnp.bfloat16)
    filled = jnp.dot(placing, normed, preferred_element_type=jnp.float32).astype(jnp.bfloat16)
    whole_rows = lax.all_gather(
        lax.all_to_all(
            filled.reshape(experts_all, 1, capacity, normed.shape[1]),
            "expert",
            split_axis=0,
            concat_axis=1,
            tiled=True,
        ),
        ("head", "pair"),
        axis=3,
        tiled=True,
    )
    expert_out = expert_block(w_gate, w_up, w_down, whole_rows)
    returned = lax.all_to_all(expert_out, "expert", split_axis=1, concat_axis=0, tiled=True)
    returned = returned.reshape(experts_all * capacity, feature_cols)
    picked = jnp.take(returned, target.reshape(-1), axis=0).reshape(tok_rows, TOPK, feature_cols)
    expert_mix = jnp.sum(route_weights[:, :, None] * picked.astype(jnp.float32), axis=1).astype(
        jnp.bfloat16
    )
    return (attn_hidden, expert_mix)


def attention_kernel(blocks, rows, heads, place, q_ref, k_ref, v_ref, wo_ref, keep_ref, send_ref, acc_ref):
    step = pl.program_id(0)
    inverse_root = 1.0 / math.sqrt(HEAD_WIDTH)
    outs = []
    for head in range(heads):
        parts = []
        for b in range(blocks):
            count = (b + 1) * rows
            q = q_ref[b * rows : count, head * HEAD_WIDTH : (head + 1) * HEAD_WIDTH]
            s = lax.dot_general(
                q, k_ref[:count, :], (((1,), (1,)), ((), ())), preferred_element_type=jnp.float32
            ) * inverse_root
            row = lax.broadcasted_iota(jnp.int32, s.shape, 0) + b * rows
            col = lax.broadcasted_iota(jnp.int32, s.shape, 1)
            s = jnp.where(col <= row, s, -jnp.inf)
            p = jnp.exp(s - jnp.max(s, axis=1, keepdims=True))
            total = jnp.sum(p, axis=1, keepdims=True)
            o = jnp.dot(p.astype(jnp.bfloat16), v_ref[:count, :], preferred_element_type=jnp.float32)
            parts.append((o / total).astype(jnp.bfloat16))
        outs.append(jnp.concatenate(parts, axis=0))
    mixed = jnp.concatenate(outs, axis=1) if heads > 1 else outs[0]
    term = jnp.dot(mixed, wo_ref[...], preferred_element_type=jnp.float32)

    @pl.when(step == 0)
    def _():
        acc_ref[...] = term

    @pl.when(step > 0)
    def _():
        acc_ref[...] += term

    @pl.when(step == pl.num_programs(0) - 1)
    def _():
        c = place[0]
        pair = place[1]
        for i in range(keep_ref.shape[0]):
            mine = pl.multiple_of((i * 2 + c) * rows, rows)
            other = pl.multiple_of((i * 2 + 1 - c) * rows, rows)
            keep_ref[i] = acc_ref[pl.ds(mine, rows), :]
            send_ref[i] = acc_ref[pl.ds(other, rows), :].astype(jnp.bfloat16)


def attend_and_project(place, gathered, wo, rows, q_cols):
    total_rows = gathered.shape[0]
    cols = wo.shape[1]
    heads = 2
    width = heads * HEAD_WIDTH
    steps = q_cols // width
    kv_at = q_cols // HEAD_WIDTH
    blocks = total_rows // rows

    def kern(place_ref, *refs):
        attention_kernel(blocks, rows, heads, place_ref, *refs)

    return pl.pallas_call(
        kern,
        out_shape=(
            jax.ShapeDtypeStruct((blocks // 2, rows, cols), jnp.float32),
            jax.ShapeDtypeStruct((blocks // 2, rows, cols), jnp.bfloat16),
        ),
        grid_spec=pltpu.PrefetchScalarGridSpec(
            num_scalar_prefetch=1,
            grid=(steps,),
            in_specs=[
                pl.BlockSpec((total_rows, width), lambda i, p: (0, i)),
                pl.BlockSpec((total_rows, HEAD_WIDTH), lambda i, p: (0, kv_at)),
                pl.BlockSpec((total_rows, HEAD_WIDTH), lambda i, p: (0, kv_at + 1)),
                pl.BlockSpec((width, cols), lambda i, p: (i, 0)),
            ],
            out_specs=(
                pl.BlockSpec((blocks // 2, rows, cols), lambda i, p: (0, 0, 0)),
                pl.BlockSpec((blocks // 2, rows, cols), lambda i, p: (0, 0, 0)),
            ),
            scratch_shapes=[pltpu.VMEM((total_rows, cols), jnp.float32)],
        ),
        name="attend",
        cost_estimate=pl.CostEstimate(
            flops=4 * total_rows * total_rows * q_cols // 2 + 2 * total_rows * q_cols * cols,
            transcendentals=total_rows * total_rows * q_cols // (2 * HEAD_WIDTH),
            bytes_accessed=2 * (gathered.size + wo.size) + 3 * total_rows * cols,
        ),
    )(place, gathered, gathered, gathered, wo)


def hidden_kernel(x_ref, gain_ref, gm_ref, go_ref, um_ref, uo_ref, place_ref, act_ref, gacc, uacc, sq):
    step = pl.program_id(0)
    rows = x_ref[0].astype(jnp.float32)
    part = jnp.sum(rows * rows, axis=1, keepdims=True)
    x = (rows * gain_ref[0]).astype(jnp.bfloat16)
    half = gm_ref.shape[1]
    terms = [
        jnp.dot(x, w[...], preferred_element_type=jnp.float32)
        for w in (gm_ref, go_ref, um_ref, uo_ref)
    ]

    @pl.when(step == 0)
    def _():
        sq[...] = jnp.broadcast_to(part, sq.shape)
        gacc[:, :half] = terms[0]
        gacc[:, half:] = terms[1]
        uacc[:, :half] = terms[2]
        uacc[:, half:] = terms[3]

    @pl.when(step > 0)
    def _():
        sq[...] += jnp.broadcast_to(part, sq.shape)
        gacc[:, :half] += terms[0]
        gacc[:, half:] += terms[1]
        uacc[:, :half] += terms[2]
        uacc[:, half:] += terms[3]

    @pl.when(step == pl.num_programs(0) - 1)
    def _():
        c = place_ref[0]
        scale = lax.rsqrt(sq[:, :1] / D + norm_eps)
        for i in range(2):
            g = gacc[:, i * half : (i + 1) * half] * scale
            u = uacc[:, i * half : (i + 1) * half] * scale
            at = pl.multiple_of((c if i == 0 else 1 - c) * half, half)
            act_ref[:, pl.ds(at, half)] = (g / (1.0 + jnp.exp(-g)) * u).astype(jnp.bfloat16)


def hidden_units(place, x, gain, wg, wg_other, wu, wu_other):
    chunks, rows, cols = x.shape
    half = wg.shape[1]
    w_spec = pl.BlockSpec((cols, half), lambda i: (i, 0))
    return pl.pallas_call(
        hidden_kernel,
        out_shape=jax.ShapeDtypeStruct((rows, 2 * half), jnp.bfloat16),
        grid=(chunks,),
        in_specs=[
            pl.BlockSpec((1, rows, cols), lambda i: (i, 0, 0)),
            pl.BlockSpec((1, 1, cols), lambda i: (i, 0, 0)),
            w_spec,
            w_spec,
            w_spec,
            w_spec,
            pl.BlockSpec(memory_space=pltpu.SMEM),
        ],
        out_specs=pl.BlockSpec((rows, 2 * half), lambda i: (0, 0)),
        scratch_shapes=[
            pltpu.VMEM((rows, 2 * half), jnp.float32),
            pltpu.VMEM((rows, 2 * half), jnp.float32),
            pltpu.VMEM((rows, LANES), jnp.float32),
        ],
        name="hidden",
        cost_estimate=pl.CostEstimate(
            flops=8 * chunks * rows * cols * half,
            transcendentals=2 * rows * half,
            bytes_accessed=2 * x.size + 8 * wg.size,
        ),
    )(x, gain, wg, wg_other, wu, wu_other, place)


def down_kernel(place_ref, a0_ref, a1_ref, b0_ref, b1_ref, w_ref, scale_ref, out_ref):
    c = place_ref[0]
    h = place_ref[1]
    half = a0_ref.shape[1]
    rows = out_ref.shape[1]
    near = w_ref[pl.ds(pl.multiple_of(h * half, half), half), :]
    far = w_ref[pl.ds(pl.multiple_of((1 - h) * half, half), half), :]
    for who, (p_ref, q_ref) in enumerate(((a0_ref, a1_ref), (b0_ref, b1_ref))):
        y = jnp.dot(p_ref[...], near, preferred_element_type=jnp.float32)
        y += jnp.dot(q_ref[...], far, preferred_element_type=jnp.float32)
        for i in range(y.shape[0] // rows):
            b = i * 2 + (c if who == 0 else 1 - c)
            out_ref[b] = (y[i * rows : (i + 1) * rows] * scale_ref[b]).astype(jnp.bfloat16)


def down_project(place, parts, w_down, scale, blocks, rows):
    cols = w_down.shape[1]
    tile = cols // 4
    full = lambda a: pl.BlockSpec(a.shape, lambda i: (0,) * a.ndim)
    return pl.pallas_call(
        down_kernel,
        out_shape=jax.ShapeDtypeStruct((blocks, rows, cols), jnp.bfloat16),
        grid=(cols // tile,),
        in_specs=[pl.BlockSpec(memory_space=pltpu.SMEM)]
        + [full(a) for a in parts]
        + [pl.BlockSpec((w_down.shape[0], tile), lambda i: (0, i)), full(scale)],
        out_specs=pl.BlockSpec((blocks, rows, tile), lambda i: (0, 0, i)),
        name="down",
        cost_estimate=pl.CostEstimate(
            flops=2 * blocks * rows * cols * w_down.shape[0],
            transcendentals=0,
            bytes_accessed=2 * w_down.size + 4 * blocks * rows * cols,
        ),
    )(place, *parts, w_down, scale)


def dense_body(sizes, resid, query, keyval, wo, norm_gain, w_gate, w_up, w_down, expert_ids, route_weights):
    E, H, C = sizes
    rows, cols = resid.shape
    q_cols = query.shape[1]

    def permute(x, move):
        perm = []
        for e in range(E):
            for h in range(H):
                for c in range(C):
                    e2, h2, c2 = move(e, h, c)
                    perm.append(((e * H + h) * C + c, ((e2 % E) * H + h2 % H) * C + c2 % C))
        return lax.ppermute(x, RING, perm)

    up = lambda x: permute(x, lambda e, h, c: (e + 1, h, c))
    down = lambda x: permute(x, lambda e, h, c: (e - 1, h, c))
    across = lambda x: permute(x, lambda e, h, c: (e, h + 1, c))
    partner = lambda x: permute(x, lambda e, h, c: (e, h, c + 1))
    swap = lambda x: permute(x, lambda e, h, c: (h * C + c, e // C, e % C))

    def ring_gather(x):
        fwd, bwd = x, x
        out = jnp.zeros((E,) + x.shape, x.dtype)
        put = lambda out, k, y: lax.dynamic_update_slice(
            out, y[None], ((e_at + k) % E,) + (0,) * y.ndim
        )
        out = put(out, 0, x)
        for k in range(1, E // 2):
            fwd, bwd = up(fwd), down(bwd)
            out = put(out, E - k, fwd)
            out = put(out, k, bwd)
        half = x.shape[0] // 2
        last = jnp.concatenate([up(fwd[:half]), down(bwd[half:])], axis=0)
        return put(out, E // 2, last)

    e_at, h_at, c_at = (lax.axis_index(a).astype(jnp.int32) for a in RING)
    place = jnp.stack([c_at, h_at]).astype(jnp.int32)

    kv = lax.dynamic_slice_in_dim(keyval, c_at * HEAD_WIDTH, HEAD_WIDTH, 2)
    experts = jnp.arange(E, dtype=jnp.int32)
    weight = jnp.sum(
        jnp.where(expert_ids[:, :, None] == experts, route_weights[:, :, None], 0.0), axis=1
    )
    high = weight.astype(jnp.bfloat16)
    low = (weight - high.astype(jnp.float32)).astype(jnp.bfloat16)
    pad = jnp.zeros((rows, LANES - 2 * E), jnp.bfloat16)
    gathered = ring_gather(jnp.concatenate([query, kv[0], kv[1], high, low, pad], axis=1))
    gathered = gathered.reshape(E * rows, -1)
    resid_here = swap(resid)
    wg, wu, wd = w_gate[0], w_up[0], w_down[0]
    wg_other, wu_other = partner(wg), partner(wu)

    keep, send = attend_and_project(place, gathered, wo, rows, q_cols)
    both = keep + partner(send).astype(jnp.float32)
    mine = lax.dynamic_index_in_dim(both, h_at, 0, keepdims=False)
    theirs = lax.dynamic_index_in_dim(both, 1 - h_at, 0, keepdims=False).astype(jnp.bfloat16)
    hidden = (
        resid_here.astype(jnp.float32) + mine + across(theirs).astype(jnp.float32)
    ).astype(jnp.bfloat16)
    attn_hidden = swap(hidden)

    other = across(hidden)
    couple = jnp.where(h_at == 0, jnp.stack([hidden, other]), jnp.stack([other, hidden]))
    x = ring_gather(couple.reshape(H * rows, cols))

    act = hidden_units(place, x, norm_gain.reshape(E, 1, cols), wg, wg_other, wu, wu_other)
    act_far = across(act)
    parts = (act, act_far, partner(act), partner(act_far))

    tail = lax.dynamic_slice_in_dim(gathered, q_cols + 2 * HEAD_WIDTH, LANES, 1).astype(jnp.float32)
    scale = lax.dynamic_slice_in_dim(tail, e_at, 1, 1) + lax.dynamic_slice_in_dim(
        tail, E + e_at, 1, 1
    )
    y = down_project(place, parts, wd, scale.reshape(E, rows, 1), E, rows)

    block = lambda k: lax.dynamic_index_in_dim(y, (e_at + k) % E, 0, keepdims=False)
    half = rows // 2
    fwd = bwd = None
    for k in range(E // 2, 0, -1):
        ahead, behind = block(k), block(E - k)
        if k == E // 2:
            ahead, behind = ahead[:half], behind[half:]
        f32 = jnp.float32
        if fwd is not None:
            if fwd.shape[0] < rows:
                fwd = jnp.concatenate([fwd, jnp.zeros_like(fwd)], axis=0)
                bwd = jnp.concatenate([jnp.zeros_like(bwd), bwd], axis=0)
            ahead = (ahead.astype(f32) + fwd.astype(f32)).astype(jnp.bfloat16)
            behind = (behind.astype(f32) + bwd.astype(f32)).astype(jnp.bfloat16)
        fwd, bwd = up(ahead), down(behind)
    mix = (block(0).astype(f32) + fwd.astype(f32) + bwd.astype(f32)).astype(jnp.bfloat16)
    return attn_hidden, mix


def body(sizes, resid, query, keyval, wo, norm_gain, w_gate, w_up, w_down, expert_ids, slot_ids, route_weights):
    E, H, C = sizes
    rows, cols = resid.shape
    capacity = 2 * rows * TOPK // (w_gate.shape[0] * E)
    dense = (
        w_gate.shape[0] == 1
        and capacity >= rows
        and H == 2
        and C == 2
        and E == H * C
        and cols == wo.shape[1]
        and keyval.shape[2] == C * HEAD_WIDTH
        and query.shape[1] * KEY_VALUE_HEADS == QUERY_HEADS * HEAD_WIDTH
        and cols * E == D
    )
    if dense:
        return dense_body(
            sizes, resid, query, keyval, wo, norm_gain, w_gate, w_up, w_down, expert_ids, route_weights
        )
    return general_body(
        resid, query, keyval, wo, norm_gain, w_gate, w_up, w_down, expert_ids, slot_ids, route_weights
    )


def solution(mesh):
    sizes = tuple(mesh.shape[a] for a in RING)
    return jax.shard_map(
        functools.partial(body, sizes),
        mesh=mesh,
        in_specs=(
            P(("groups", "expert"), ("head", "pair")),
            P(("groups", "expert"), ("head", "pair")),
            P(None, ("groups", "expert"), "head"),
            P(("head", "pair"), "expert"),
            P(),
            P("expert", None, ("head", "pair")),
            P("expert", None, ("head", "pair")),
            P("expert", None, ("head", "pair")),
            P(("groups", "expert"), None),
            P(("groups", "expert"), None),
            P(("groups", "expert"), None),
        ),
        out_specs=(
            P(("groups", "expert"), ("head", "pair")),
            P(("groups", "expert"), ("head", "pair")),
        ),
        check_vma=False,
    )
```

```python
import functools
import math

import jax
import jax.numpy as jnp
from jax import lax
from jax.experimental import pallas as pl
from jax.experimental.pallas import tpu as pltpu
from jax.sharding import PartitionSpec as P

D = 4096
QUERY_HEADS = 32
KEY_VALUE_HEADS = 4
HEAD_WIDTH = 128
TOPK = 2
LANES = 128

norm_eps = 1e-06
RING = ("expert", "head", "pair")


def expert_block(w_gate, w_up, w_down, slot_block):
    gate_val = jnp.einsum("ensd,edf->ensf", slot_block, w_gate, preferred_element_type=jnp.float32)
    up_val = jnp.einsum("ensd,edf->ensf", slot_block, w_up, preferred_element_type=jnp.float32)
    activated = (jax.nn.silu(gate_val) * up_val).astype(jnp.bfloat16)
    all_hidden = lax.all_gather(activated, ("head", "pair"), axis=3, tiled=True)
    return jnp.einsum(
        "ensf,efd->ensd", all_hidden, w_down, preferred_element_type=jnp.float32
    ).astype(jnp.bfloat16)


def general_body(
    resid, query, keyval, wo, norm_gain, w_gate, w_up, w_down, expert_ids, slot_ids, route_weights
):
    tok_rows = resid.shape[0]
    feature_cols = resid.shape[1]
    q_local = query.shape[1] // HEAD_WIDTH
    kv_local = keyval.shape[2] // HEAD_WIDTH
    heads_per_group = QUERY_HEADS // KEY_VALUE_HEADS
    query_pos = lax.axis_index("expert") * tok_rows + jnp.arange(tok_rows, dtype=jnp.int32)
    key_head = (
        lax.axis_index("pair") * q_local + jnp.arange(q_local, dtype=jnp.int32)
    ) // heads_per_group
    queries = query.reshape(tok_rows, q_local, HEAD_WIDTH)
    inverse_root = 1.0 / math.sqrt(HEAD_WIDTH)
    shards = lax.all_gather(keyval, "expert", axis=1, tiled=True)
    run_max = jnp.full((tok_rows, q_local), -1e30, jnp.float32)
    count = shards.shape[1]
    keys_here = jnp.take(shards[0].reshape(count, kv_local, HEAD_WIDTH), key_head, axis=1)
    values_here = jnp.take(shards[1].reshape(count, kv_local, HEAD_WIDTH), key_head, axis=1)
    scores = (
        jnp.einsum("thd,uhd->thu", queries, keys_here, preferred_element_type=jnp.float32)
        * inverse_root
    )
    key_pos = jnp.arange(count, dtype=jnp.int32)
    visible = (key_pos[None, :] <= query_pos[:, None])[:, None, :]
    scores = jnp.where(visible, scores, -jnp.inf)
    new_max = jnp.maximum(run_max, jnp.max(scores, axis=2))
    weights = jnp.where(visible, jnp.exp(scores - new_max[:, :, None]), 0.0)
    run_total = jnp.sum(weights, axis=2)
    weighted = jnp.einsum(
        "thu,uhd->thd",
        weights.astype(jnp.bfloat16),
        values_here,
        preferred_element_type=jnp.float32,
    )
    heads_out = (
        (weighted / run_total[:, :, None])
        .astype(jnp.bfloat16)
        .reshape(tok_rows, q_local * HEAD_WIDTH)
    )
    partial_proj = jnp.dot(
        heads_out,
        lax.all_gather(wo, "expert", axis=1, tiled=True),
        preferred_element_type=jnp.float32,
    )
    attn_sum = lax.psum_scatter(
        partial_proj.astype(jnp.bfloat16), ("head", "pair"), scatter_dimension=1, tiled=True
    ).astype(jnp.float32)
    attn_hidden = (resid.astype(jnp.float32) + attn_sum).astype(jnp.bfloat16)
    experts_here = w_gate.shape[0]
    experts_all = experts_here * lax.axis_size("expert")
    capacity = 2 * tok_rows * TOPK // experts_all
    target = expert_ids * capacity + slot_ids
    slot_index = jnp.arange(experts_all * capacity, dtype=jnp.int32)
    placing = jnp.sum(
        (target[None, :, :] == slot_index[:, None, None]).astype(jnp.int32), axis=2
    ).astype(jnp.bfloat16)
    row_floats = attn_hidden.astype(jnp.float32)
    square_sum = lax.psum(jnp.sum(row_floats * row_floats, axis=1), ("head", "pair"))
    mean_square = (square_sum / D)[:, None]
    shard_index = lax.axis_index("head") * lax.axis_size("pair") + lax.axis_index("pair")
    gain_part = lax.dynamic_slice_in_dim(norm_gain, shard_index * feature_cols, feature_cols)
    normed = (row_floats * lax.rsqrt(mean_square + norm_eps) * gain_part).astype(jnp.bfloat16)
    filled = jnp.dot(placing, normed, preferred_element_type=jnp.float32).astype(jnp.bfloat16)
    whole_rows = lax.all_gather(
        lax.all_to_all(
            filled.reshape(experts_all, 1, capacity, normed.shape[1]),
            "expert",
            split_axis=0,
            concat_axis=1,
            tiled=True,
        ),
        ("head", "pair"),
        axis=3,
        tiled=True,
    )
    expert_out = expert_block(w_gate, w_up, w_down, whole_rows)
    returned = lax.all_to_all(expert_out, "expert", split_axis=1, concat_axis=0, tiled=True)
    returned = returned.reshape(experts_all * capacity, feature_cols)
    picked = jnp.take(returned, target.reshape(-1), axis=0).reshape(tok_rows, TOPK, feature_cols)
    expert_mix = jnp.sum(route_weights[:, :, None] * picked.astype(jnp.float32), axis=1).astype(
        jnp.bfloat16
    )
    return (attn_hidden, expert_mix)


def vmem():
    return pl.BlockSpec(memory_space=pltpu.VMEM)


def smem():
    return pl.BlockSpec(memory_space=pltpu.SMEM)


def attend(place, slot, q, kvs, wo):
    rows, q_cols = q.shape
    cols = wo.shape[1]
    heads = q_cols // HEAD_WIDTH
    scale = 1.0 / math.sqrt(HEAD_WIDTH)

    def kern(place_ref, q_ref, *refs):
        kv_refs, (wo_ref, out_ref) = refs[: len(kvs)], refs[len(kvs) :]
        e = place_ref[0]
        row = lax.broadcasted_iota(jnp.int32, (rows, rows), 0)
        col = lax.broadcasted_iota(jnp.int32, (rows, rows), 1)
        bias = []
        for i in range(len(kvs)):
            if i == slot:
                bias.append(jnp.where(col <= row, 0.0, -jnp.inf).astype(jnp.float32))
            else:
                seen = (e ^ i) < (e ^ slot)
                bias.append(jnp.full((1, rows), jnp.where(seen, 0.0, -jnp.inf), jnp.float32))
        outs = []
        for head in range(heads):
            qh = q_ref[:, head * HEAD_WIDTH : (head + 1) * HEAD_WIDTH]
            scores = [
                lax.dot_general(
                    qh, kv[:, :HEAD_WIDTH], (((1,), (1,)), ((), ())), preferred_element_type=jnp.float32
                )
                * scale
                + bias[i]
                for i, kv in enumerate(kv_refs)
            ]
            top = functools.reduce(jnp.maximum, scores)
            top = jnp.max(top, axis=1, keepdims=True)
            probs = [jnp.exp(s - top) for s in scores]
            total = jnp.sum(functools.reduce(jnp.add, probs), axis=1, keepdims=True)
            mixed = functools.reduce(
                jnp.add,
                [
                    jnp.dot(
                        p.astype(jnp.bfloat16), kv[:, HEAD_WIDTH:], preferred_element_type=jnp.float32
                    )
                    for p, kv in zip(probs, kv_refs)
                ],
            )
            outs.append((mixed / total).astype(jnp.bfloat16))
        mixed = jnp.concatenate(outs, axis=1)
        out_ref[...] = jnp.dot(mixed, wo_ref[...], preferred_element_type=jnp.float32)

    return pl.pallas_call(
        kern,
        out_shape=jax.ShapeDtypeStruct((rows, cols), jnp.float32),
        in_specs=[smem()] + [vmem()] * (2 + len(kvs)),
        out_specs=vmem(),
        name=f"attend{slot}",
        cost_estimate=pl.CostEstimate(
            flops=4 * rows * rows * len(kvs) * q_cols + 2 * rows * q_cols * cols,
            transcendentals=rows * rows * len(kvs) * heads,
            bytes_accessed=2 * (q.size + wo.size) + 4 * rows * cols,
        ),
    )(place, q, *kvs, wo)


def hidden_units(place, xs, slots, gain, weights, carry, last):
    rows, cols = xs[0][0].shape
    half = weights[0].shape[1]
    tokens = 2 * rows

    def kern(place_ref, *refs):
        refs = list(refs)
        x_refs = [(refs.pop(0), refs.pop(0)) for _ in xs]
        gain_ref = refs.pop(0)
        w_refs = [refs.pop(0) for _ in weights]
        carry_refs = [refs.pop(0) for _ in carry]
        e, c = place_ref[0], place_ref[2]
        sums = [r[...] for r in carry_refs]
        for slot, (mine, other) in zip(slots, x_refs):
            at = e ^ slot
            x = jnp.concatenate([mine[...], other[...]], axis=0).astype(jnp.float32)
            part = [jnp.broadcast_to(jnp.sum(x * x, axis=1, keepdims=True), (tokens, LANES))]
            x = (x * gain_ref[at]).astype(jnp.bfloat16)
            at = pl.multiple_of(at * cols, cols)
            for w in w_refs:
                part.append(jnp.dot(x, w[pl.ds(at, cols), :], preferred_element_type=jnp.float32))
            sums = [a + b for a, b in zip(sums, part)] if sums else part
        if not last:
            for out, s in zip(refs, sums):
                out[...] = s
            return
        act_ref = refs[0]
        scale = lax.rsqrt(sums[0][:, :1] / D + norm_eps)
        for i in range(2):
            g = sums[1 + i] * scale
            u = sums[3 + i] * scale
            at = pl.multiple_of((c if i == 0 else 1 - c) * half, half)
            act_ref[:, pl.ds(at, half)] = (g / (1.0 + jnp.exp(-g)) * u).astype(jnp.bfloat16)

    f32 = jnp.float32
    if last:
        out_shape = jax.ShapeDtypeStruct((tokens, 2 * half), jnp.bfloat16)
        out_specs = vmem()
    else:
        out_shape = [jax.ShapeDtypeStruct((tokens, LANES), f32)] + [
            jax.ShapeDtypeStruct((tokens, half), f32) for _ in weights
        ]
        out_specs = [vmem()] * len(out_shape)
    flat = [a for pair in xs for a in pair]
    return pl.pallas_call(
        kern,
        out_shape=out_shape,
        in_specs=[smem()] + [vmem()] * (len(flat) + 1 + len(weights) + len(carry)),
        out_specs=out_specs,
        name="hidden" + "".join(str(s) for s in slots),
        cost_estimate=pl.CostEstimate(
            flops=8 * len(xs) * tokens * cols * half,
            transcendentals=2 * tokens * half if last else 0,
            bytes_accessed=len(xs) * (2 * tokens * cols + 8 * cols * half),
        ),
    )(place, *flat, gain, *weights, *carry)


def down_project(place, parts, w_down):
    rows = parts[0].shape[0] // 2
    half = parts[0].shape[1]
    cols = w_down.shape[1]
    blocks = 4

    def kern(place_ref, a0, a1, b0, b1, w_ref, out_ref):
        e, h, c = place_ref[0], place_ref[1], place_ref[2]
        near = w_ref[pl.ds(pl.multiple_of(h * half, half), half), :]
        far = w_ref[pl.ds(pl.multiple_of((1 - h) * half, half), half), :]
        for who, (p_ref, q_ref) in enumerate(((a0, a1), (b0, b1))):
            q = jnp.concatenate([q_ref[rows:, :], q_ref[:rows, :]], axis=0)
            y = jnp.dot(p_ref[...], near, preferred_element_type=jnp.float32)
            y += jnp.dot(q, far, preferred_element_type=jnp.float32)
            for i in range(2):
                block = 2 * (h if i == 0 else 1 - h) + (c if who == 0 else 1 - c)
                out_ref[block ^ e] = y[i * rows : (i + 1) * rows].astype(jnp.bfloat16)

    return pl.pallas_call(
        kern,
        out_shape=jax.ShapeDtypeStruct((blocks, rows, cols), jnp.bfloat16),
        in_specs=[smem()] + [vmem()] * 5,
        out_specs=vmem(),
        name="down",
        cost_estimate=pl.CostEstimate(
            flops=2 * blocks * rows * cols * w_down.shape[0],
            transcendentals=0,
            bytes_accessed=2 * w_down.size + 4 * blocks * rows * cols,
        ),
    )(place, *parts, w_down)


def dense_body(sizes, resid, query, keyval, wo, norm_gain, w_gate, w_up, w_down, expert_ids, route_weights):
    E, H, C = sizes
    rows, cols = resid.shape
    f32 = jnp.float32
    bf16 = jnp.bfloat16

    def permute(x, name, move):
        perm = []
        for e in range(E):
            for h in range(H):
                for c in range(C):
                    e2, h2, c2 = move(e, h, c)
                    perm.append(((e * H + h) * C + c, (e2 * H + h2) * C + c2))
        with jax.named_scope(name):
            return lax.ppermute(x, RING, perm)

    hop = lambda x, k, name: permute(x, name + str(k), lambda e, h, c: (e ^ k, h, c))
    across = lambda x, name: permute(x, name, lambda e, h, c: (e, 1 - h, c))
    partner = lambda x, name: permute(x, name, lambda e, h, c: (e, h, 1 - c))
    swap = lambda x, name: permute(x, name, lambda e, h, c: (h * C + c, e // C, e % C))

    e_at, h_at, c_at = (lax.axis_index(a).astype(jnp.int32) for a in RING)
    place = jnp.stack([e_at, h_at, c_at])
    far_slots = range(1, E)

    own_kv = lax.dynamic_slice_in_dim(keyval, c_at * HEAD_WIDTH, HEAD_WIDTH, 2)
    own_kv = jnp.concatenate([own_kv[0], own_kv[1]], axis=1)
    kvs = [own_kv] + [hop(own_kv, k, "kv") for k in far_slots]
    qs = [query] + [hop(query, k, "q") for k in far_slots]
    wg, wu, wd = w_gate[0], w_up[0], w_down[0]
    wg_other, wu_other = partner(wg, "wg"), partner(wu, "wu")
    resid_here = swap(resid, "resid")

    terms = [attend(place, k, qs[k], kvs, wo) for k in range(E)]
    even = (e_at % C) == c_at
    sums = []
    for first, second in ((0, 1), (2, 3)):
        keep = jnp.where(even, terms[first], terms[second])
        send = jnp.where(even, terms[second], terms[first]).astype(bf16)
        sums.append(keep + partner(send, f"pair{first}").astype(f32))
    at_home = (e_at // C) == h_at
    mine = jnp.where(at_home, sums[0], sums[1])
    theirs = jnp.where(at_home, sums[1], sums[0]).astype(bf16)
    hidden = (resid_here.astype(f32) + mine + across(theirs, "cross").astype(f32)).astype(bf16)
    attn_hidden = swap(hidden, "home")

    cuts = [hidden] + [hop(hidden, k, "feat") for k in far_slots]
    xs = [(x, across(x, f"fx{k}")) for k, x in enumerate(cuts)]
    gain = norm_gain.reshape(E, 1, cols)
    weights = (wg, wg_other, wu, wu_other)
    carry = hidden_units(place, xs[:2], (0, 1), gain, weights, (), False)
    act = hidden_units(place, xs[2:], (2, 3), gain, weights, carry, True)
    act_far = across(act, "actx")
    parts = (act, act_far, partner(act, "actp"), partner(act_far, "actq"))
    y = down_project(place, parts, wd)

    mix = jnp.zeros((rows, cols), f32)
    for k in range(E):
        got = y[0] if k == 0 else hop(y[k], k, "out")
        weight = jnp.sum(jnp.where(expert_ids == (e_at ^ k), route_weights, 0.0), axis=1, keepdims=True)
        mix += weight * got.astype(f32)
    return attn_hidden, mix.astype(bf16)


def body(sizes, resid, query, keyval, wo, norm_gain, w_gate, w_up, w_down, expert_ids, slot_ids, route_weights):
    E, H, C = sizes
    rows, cols = resid.shape
    capacity = 2 * rows * TOPK // (w_gate.shape[0] * E)
    dense = (
        w_gate.shape[0] == 1
        and capacity >= rows
        and H == 2
        and C == 2
        and E == H * C
        and cols == wo.shape[1]
        and keyval.shape[2] == C * HEAD_WIDTH
        and query.shape[1] * KEY_VALUE_HEADS == QUERY_HEADS * HEAD_WIDTH
        and cols * E == D
    )
    if dense:
        return dense_body(
            sizes, resid, query, keyval, wo, norm_gain, w_gate, w_up, w_down, expert_ids, route_weights
        )
    return general_body(
        resid, query, keyval, wo, norm_gain, w_gate, w_up, w_down, expert_ids, slot_ids, route_weights
    )


def solution(mesh):
    sizes = tuple(mesh.shape[a] for a in RING)
    return jax.shard_map(
        functools.partial(body, sizes),
        mesh=mesh,
        in_specs=(
            P(("groups", "expert"), ("head", "pair")),
            P(("groups", "expert"), ("head", "pair")),
            P(None, ("groups", "expert"), "head"),
            P(("head", "pair"), "expert"),
            P(),
            P("expert", None, ("head", "pair")),
            P("expert", None, ("head", "pair")),
            P("expert", None, ("head", "pair")),
            P(("groups", "expert"), None),
            P(("groups", "expert"), None),
            P(("groups", "expert"), None),
        ),
        out_specs=(
            P(("groups", "expert"), ("head", "pair")),
            P(("groups", "expert"), ("head", "pair")),
        ),
        check_vma=False,
    )
```

```python
import functools
import math

import jax
import jax.numpy as jnp
from jax import lax
from jax.experimental import pallas as pl
from jax.experimental.pallas import tpu as pltpu
from jax.sharding import PartitionSpec as P

D = 4096
QUERY_HEADS = 32
KEY_VALUE_HEADS = 4
HEAD_WIDTH = 128
TOPK = 2
LANES = 128
ATTEND_VMEM = 6 << 20
HIDDEN_VMEM = 10 << 20
DOWN_VMEM = 10 << 20

norm_eps = 1e-06
RING = ("expert", "head", "pair")


def expert_block(w_gate, w_up, w_down, slot_block):
    gate_val = jnp.einsum("ensd,edf->ensf", slot_block, w_gate, preferred_element_type=jnp.float32)
    up_val = jnp.einsum("ensd,edf->ensf", slot_block, w_up, preferred_element_type=jnp.float32)
    activated = (jax.nn.silu(gate_val) * up_val).astype(jnp.bfloat16)
    all_hidden = lax.all_gather(activated, ("head", "pair"), axis=3, tiled=True)
    return jnp.einsum(
        "ensf,efd->ensd", all_hidden, w_down, preferred_element_type=jnp.float32
    ).astype(jnp.bfloat16)


def general_body(
    resid, query, keyval, wo, norm_gain, w_gate, w_up, w_down, expert_ids, slot_ids, route_weights
):
    tok_rows = resid.shape[0]
    feature_cols = resid.shape[1]
    q_local = query.shape[1] // HEAD_WIDTH
    kv_local = keyval.shape[2] // HEAD_WIDTH
    heads_per_group = QUERY_HEADS // KEY_VALUE_HEADS
    query_pos = lax.axis_index("expert") * tok_rows + jnp.arange(tok_rows, dtype=jnp.int32)
    key_head = (
        lax.axis_index("pair") * q_local + jnp.arange(q_local, dtype=jnp.int32)
    ) // heads_per_group
    queries = query.reshape(tok_rows, q_local, HEAD_WIDTH)
    inverse_root = 1.0 / math.sqrt(HEAD_WIDTH)
    shards = lax.all_gather(keyval, "expert", axis=1, tiled=True)
    run_max = jnp.full((tok_rows, q_local), -1e30, jnp.float32)
    count = shards.shape[1]
    keys_here = jnp.take(shards[0].reshape(count, kv_local, HEAD_WIDTH), key_head, axis=1)
    values_here = jnp.take(shards[1].reshape(count, kv_local, HEAD_WIDTH), key_head, axis=1)
    scores = (
        jnp.einsum("thd,uhd->thu", queries, keys_here, preferred_element_type=jnp.float32)
        * inverse_root
    )
    key_pos = jnp.arange(count, dtype=jnp.int32)
    visible = (key_pos[None, :] <= query_pos[:, None])[:, None, :]
    scores = jnp.where(visible, scores, -jnp.inf)
    new_max = jnp.maximum(run_max, jnp.max(scores, axis=2))
    weights = jnp.where(visible, jnp.exp(scores - new_max[:, :, None]), 0.0)
    run_total = jnp.sum(weights, axis=2)
    weighted = jnp.einsum(
        "thu,uhd->thd",
        weights.astype(jnp.bfloat16),
        values_here,
        preferred_element_type=jnp.float32,
    )
    heads_out = (
        (weighted / run_total[:, :, None])
        .astype(jnp.bfloat16)
        .reshape(tok_rows, q_local * HEAD_WIDTH)
    )
    partial_proj = jnp.dot(
        heads_out,
        lax.all_gather(wo, "expert", axis=1, tiled=True),
        preferred_element_type=jnp.float32,
    )
    attn_sum = lax.psum_scatter(
        partial_proj.astype(jnp.bfloat16), ("head", "pair"), scatter_dimension=1, tiled=True
    ).astype(jnp.float32)
    attn_hidden = (resid.astype(jnp.float32) + attn_sum).astype(jnp.bfloat16)
    experts_here = w_gate.shape[0]
    experts_all = experts_here * lax.axis_size("expert")
    capacity = 2 * tok_rows * TOPK // experts_all
    target = expert_ids * capacity + slot_ids
    slot_index = jnp.arange(experts_all * capacity, dtype=jnp.int32)
    placing = jnp.sum(
        (target[None, :, :] == slot_index[:, None, None]).astype(jnp.int32), axis=2
    ).astype(jnp.bfloat16)
    row_floats = attn_hidden.astype(jnp.float32)
    square_sum = lax.psum(jnp.sum(row_floats * row_floats, axis=1), ("head", "pair"))
    mean_square = (square_sum / D)[:, None]
    shard_index = lax.axis_index("head") * lax.axis_size("pair") + lax.axis_index("pair")
    gain_part = lax.dynamic_slice_in_dim(norm_gain, shard_index * feature_cols, feature_cols)
    normed = (row_floats * lax.rsqrt(mean_square + norm_eps) * gain_part).astype(jnp.bfloat16)
    filled = jnp.dot(placing, normed, preferred_element_type=jnp.float32).astype(jnp.bfloat16)
    whole_rows = lax.all_gather(
        lax.all_to_all(
            filled.reshape(experts_all, 1, capacity, normed.shape[1]),
            "expert",
            split_axis=0,
            concat_axis=1,
            tiled=True,
        ),
        ("head", "pair"),
        axis=3,
        tiled=True,
    )
    expert_out = expert_block(w_gate, w_up, w_down, whole_rows)
    returned = lax.all_to_all(expert_out, "expert", split_axis=1, concat_axis=0, tiled=True)
    returned = returned.reshape(experts_all * capacity, feature_cols)
    picked = jnp.take(returned, target.reshape(-1), axis=0).reshape(tok_rows, TOPK, feature_cols)
    expert_mix = jnp.sum(route_weights[:, :, None] * picked.astype(jnp.float32), axis=1).astype(
        jnp.bfloat16
    )
    return (attn_hidden, expert_mix)


def vmem():
    return pl.BlockSpec(memory_space=pltpu.VMEM)


def smem():
    return pl.BlockSpec(memory_space=pltpu.SMEM)


def attend(place, slot, q, kvs, wo, prior=None):
    rows, q_cols = q.shape
    cols = wo.shape[1]
    heads = q_cols // HEAD_WIDTH
    scale = 1.0 / math.sqrt(HEAD_WIDTH)
    extra = () if prior is None else (prior,)

    def kern(place_ref, q_ref, *refs):
        kv_refs, wo_ref, refs = refs[: len(kvs)], refs[len(kvs)], refs[len(kvs) + 1 :]
        e, c = place_ref[0], place_ref[2]
        row = lax.broadcasted_iota(jnp.int32, (rows, rows), 0)
        col = lax.broadcasted_iota(jnp.int32, (rows, rows), 1)
        bias = []
        for i in range(len(kvs)):
            if i == slot:
                bias.append(jnp.where(col <= row, 0.0, -jnp.inf).astype(jnp.float32))
            else:
                seen = (e ^ i) < (e ^ slot)
                bias.append(jnp.full((1, rows), jnp.where(seen, 0.0, -jnp.inf), jnp.float32))
        outs = []
        for head in range(heads):
            qh = q_ref[:, head * HEAD_WIDTH : (head + 1) * HEAD_WIDTH]
            scores = [
                lax.dot_general(
                    qh, kv[:, :HEAD_WIDTH], (((1,), (1,)), ((), ())), preferred_element_type=jnp.float32
                )
                * scale
                + bias[i]
                for i, kv in enumerate(kv_refs)
            ]
            top = functools.reduce(jnp.maximum, scores)
            top = jnp.max(top, axis=1, keepdims=True)
            probs = [jnp.exp(s - top) for s in scores]
            total = jnp.sum(functools.reduce(jnp.add, probs), axis=1, keepdims=True)
            mixed = functools.reduce(
                jnp.add,
                [
                    jnp.dot(
                        p.astype(jnp.bfloat16), kv[:, HEAD_WIDTH:], preferred_element_type=jnp.float32
                    )
                    for p, kv in zip(probs, kv_refs)
                ],
            )
            outs.append((mixed / total).astype(jnp.bfloat16))
        mixed = jnp.concatenate(outs, axis=1)
        term = jnp.dot(mixed, wo_ref[...], preferred_element_type=jnp.float32)
        if prior is None:
            refs[0][...] = term
            return
        prior_ref, keep_ref, send_ref = refs
        even = e % 2 == c

        @pl.when(even)
        def _():
            keep_ref[...] = prior_ref[...]
            send_ref[...] = term.astype(jnp.bfloat16)

        @pl.when(jnp.logical_not(even))
        def _():
            keep_ref[...] = term
            send_ref[...] = prior_ref[...].astype(jnp.bfloat16)

    out_shape = [jax.ShapeDtypeStruct((rows, cols), jnp.float32)]
    if extra:
        out_shape.append(jax.ShapeDtypeStruct((rows, cols), jnp.bfloat16))
    return pl.pallas_call(
        kern,
        out_shape=out_shape,
        in_specs=[smem()] + [vmem()] * (2 + len(kvs) + len(extra)),
        out_specs=[vmem()] * len(out_shape),
        name="attend",
        compiler_params=pltpu.CompilerParams(vmem_limit_bytes=ATTEND_VMEM),
        cost_estimate=pl.CostEstimate(
            flops=4 * rows * rows * len(kvs) * q_cols + 2 * rows * q_cols * cols,
            transcendentals=rows * rows * len(kvs) * heads,
            bytes_accessed=2 * (q.size + wo.size) + 4 * rows * cols,
        ),
    )(place, q, *kvs, wo, *extra)


def hidden_units(place, xs, slots, gain, weights, carry, last):
    rows, cols = xs[0][0].shape
    half = weights[0].shape[1]
    tokens = 2 * rows

    def kern(place_ref, *refs):
        refs = list(refs)
        x_refs = [(refs.pop(0), refs.pop(0)) for _ in xs]
        gain_ref = refs.pop(0)
        w_refs = [refs.pop(0) for _ in weights]
        carry_refs = [refs.pop(0) for _ in carry]
        e, c = place_ref[0], place_ref[2]
        sums = [r[...] for r in carry_refs]
        for slot, (mine, other) in zip(slots, x_refs):
            at = e ^ slot
            x = jnp.concatenate([mine[...], other[...]], axis=0).astype(jnp.float32)
            part = [jnp.broadcast_to(jnp.sum(x * x, axis=1, keepdims=True), (tokens, LANES))]
            x = (x * gain_ref[at]).astype(jnp.bfloat16)
            at = pl.multiple_of(at * cols, cols)
            for w in w_refs:
                part.append(jnp.dot(x, w[pl.ds(at, cols), :], preferred_element_type=jnp.float32))
            sums = [a + b for a, b in zip(sums, part)] if sums else part
        if not last:
            for out, s in zip(refs, sums):
                out[...] = s
            return
        act_ref = refs[0]
        scale = lax.rsqrt(sums[0][:, :1] / D + norm_eps)
        for i in range(2):
            g = sums[1 + i] * scale
            u = sums[3 + i] * scale
            at = pl.multiple_of((c if i == 0 else 1 - c) * half, half)
            act_ref[:, pl.ds(at, half)] = (g / (1.0 + jnp.exp(-g)) * u).astype(jnp.bfloat16)

    f32 = jnp.float32
    if last:
        out_shape = jax.ShapeDtypeStruct((tokens, 2 * half), jnp.bfloat16)
        out_specs = vmem()
    else:
        out_shape = [jax.ShapeDtypeStruct((tokens, LANES), f32)] + [
            jax.ShapeDtypeStruct((tokens, half), f32) for _ in weights
        ]
        out_specs = [vmem()] * len(out_shape)
    flat = [a for pair in xs for a in pair]
    return pl.pallas_call(
        kern,
        out_shape=out_shape,
        in_specs=[smem()] + [vmem()] * (len(flat) + 1 + len(weights) + len(carry)),
        out_specs=out_specs,
        name="hidden",
        compiler_params=pltpu.CompilerParams(vmem_limit_bytes=HIDDEN_VMEM),
        cost_estimate=pl.CostEstimate(
            flops=8 * len(xs) * tokens * cols * half,
            transcendentals=2 * tokens * half if last else 0,
            bytes_accessed=len(xs) * (2 * tokens * cols + 8 * cols * half),
        ),
    )(place, *flat, gain, *weights, *carry)


def down_project(place, parts, w_down):
    rows = parts[0].shape[0] // 2
    half = parts[0].shape[1]
    cols = w_down.shape[1]
    blocks = 4

    def kern(place_ref, a0, a1, b0, b1, w_ref, out_ref):
        e, h, c = place_ref[0], place_ref[1], place_ref[2]
        near = w_ref[pl.ds(pl.multiple_of(h * half, half), half), :]
        far = w_ref[pl.ds(pl.multiple_of((1 - h) * half, half), half), :]
        for who, (p_ref, q_ref) in enumerate(((a0, a1), (b0, b1))):
            q = jnp.concatenate([q_ref[rows:, :], q_ref[:rows, :]], axis=0)
            y = jnp.dot(p_ref[...], near, preferred_element_type=jnp.float32)
            y += jnp.dot(q, far, preferred_element_type=jnp.float32)
            for i in range(2):
                block = 2 * (h if i == 0 else 1 - h) + (c if who == 0 else 1 - c)
                out_ref[block ^ e] = y[i * rows : (i + 1) * rows].astype(jnp.bfloat16)

    return pl.pallas_call(
        kern,
        out_shape=jax.ShapeDtypeStruct((blocks, rows, cols), jnp.bfloat16),
        in_specs=[smem()] + [vmem()] * 5,
        out_specs=vmem(),
        name="down",
        compiler_params=pltpu.CompilerParams(vmem_limit_bytes=DOWN_VMEM),
        cost_estimate=pl.CostEstimate(
            flops=2 * blocks * rows * cols * w_down.shape[0],
            transcendentals=0,
            bytes_accessed=2 * w_down.size + 4 * blocks * rows * cols,
        ),
    )(place, *parts, w_down)


def dense_body(sizes, resid, query, keyval, wo, norm_gain, w_gate, w_up, w_down, expert_ids, route_weights):
    E, H, C = sizes
    rows, cols = resid.shape
    f32 = jnp.float32
    bf16 = jnp.bfloat16

    def permute(x, move):
        perm = []
        for e in range(E):
            for h in range(H):
                for c in range(C):
                    e2, h2, c2 = move(e, h, c)
                    perm.append(((e * H + h) * C + c, (e2 * H + h2) * C + c2))
        return lax.ppermute(x, RING, perm)

    hop = lambda x, k: permute(x, lambda e, h, c: (e ^ k, h, c))
    across = lambda x: permute(x, lambda e, h, c: (e, 1 - h, c))
    partner = lambda x: permute(x, lambda e, h, c: (e, h, 1 - c))
    swap = lambda x: permute(x, lambda e, h, c: (h * C + c, e // C, e % C))

    e_at, h_at, c_at = (lax.axis_index(a).astype(jnp.int32) for a in RING)
    place = jnp.stack([e_at, h_at, c_at])
    far_slots = range(1, E)

    own_kv = lax.dynamic_slice_in_dim(keyval, c_at * HEAD_WIDTH, HEAD_WIDTH, 2)
    own_kv = jnp.concatenate([own_kv[0], own_kv[1]], axis=1)
    kvs = [own_kv] + [hop(own_kv, k) for k in far_slots]
    qs = [query] + [hop(query, k) for k in far_slots]
    wg, wu, wd = w_gate[0], w_up[0], w_down[0]
    wg_other, wu_other = partner(wg), partner(wu)
    resid_here = swap(resid)

    sums = []
    for first, second in ((0, 1), (2, 3)):
        prior = attend(place, first, qs[first], kvs, wo)[0]
        keep, send = attend(place, second, qs[second], kvs, wo, prior)
        sums.append(keep + partner(send).astype(f32))
    at_home = (e_at // C) == h_at
    mine = jnp.where(at_home, sums[0], sums[1])
    theirs = jnp.where(at_home, sums[1], sums[0]).astype(bf16)
    hidden = (resid_here.astype(f32) + mine + across(theirs).astype(f32)).astype(bf16)
    attn_hidden = swap(hidden)

    cuts = [hidden] + [hop(hidden, k) for k in far_slots]
    xs = [(x, across(x)) for x in cuts]
    gain = norm_gain.reshape(E, 1, cols)
    weights = (wg, wg_other, wu, wu_other)
    carry = ()
    for k in range(E):
        carry = hidden_units(place, xs[k : k + 1], (k,), gain, weights, carry, k == E - 1)
    act = carry
    act_far = across(act)
    parts = (act, act_far, partner(act), partner(act_far))
    y = down_project(place, parts, wd)

    mix = jnp.zeros((rows, cols), f32)
    for k in range(E):
        got = y[0] if k == 0 else hop(y[k], k)
        weight = jnp.sum(jnp.where(expert_ids == (e_at ^ k), route_weights, 0.0), axis=1, keepdims=True)
        mix += weight * got.astype(f32)
    return attn_hidden, mix.astype(bf16)


def body_of(sizes, resid, query, keyval, wo, norm_gain, w_gate, w_up, w_down, expert_ids, slot_ids, route_weights):
    E, H, C = sizes
    rows, cols = resid.shape
    capacity = 2 * rows * TOPK // (w_gate.shape[0] * E)
    dense = (
        w_gate.shape[0] == 1
        and capacity >= rows
        and H == 2
        and C == 2
        and E == H * C
        and cols == wo.shape[1]
        and keyval.shape[2] == C * HEAD_WIDTH
        and query.shape[1] * KEY_VALUE_HEADS == QUERY_HEADS * HEAD_WIDTH
        and cols * E == D
    )
    if dense:
        return dense_body(sizes, resid, query, keyval, wo, norm_gain, w_gate, w_up, w_down, expert_ids, route_weights)
    return general_body(
        resid, query, keyval, wo, norm_gain, w_gate, w_up, w_down, expert_ids, slot_ids, route_weights
    )


def body(sizes, *args):
    return body_of(sizes, *args)


def solution(mesh):
    sizes = tuple(mesh.shape[a] for a in RING)
    return jax.shard_map(
        functools.partial(body, sizes),
        mesh=mesh,
        in_specs=(
            P(("groups", "expert"), ("head", "pair")),
            P(("groups", "expert"), ("head", "pair")),
            P(None, ("groups", "expert"), "head"),
            P(("head", "pair"), "expert"),
            P(),
            P("expert", None, ("head", "pair")),
            P("expert", None, ("head", "pair")),
            P("expert", None, ("head", "pair")),
            P(("groups", "expert"), None),
            P(("groups", "expert"), None),
            P(("groups", "expert"), None),
        ),
        out_specs=(
            P(("groups", "expert"), ("head", "pair")),
            P(("groups", "expert"), ("head", "pair")),
        ),
        check_vma=False,
    )
```
